32 devices in a mesh: occ: 8 (over z, x), aux: 4 (over y, core).
Axes of the slice: x: 2, y: 2, z: 4, core: 2. Of those that a mesh axis runs over, the one named last changes fastest.
Arguments:
- three_index: bfloat16 [8, 448, 1536], P('occ', None, 'aux'), may hold values from -0.75 to 0.75
- occ_energy: float32 [8], P('occ'), may hold values from -2 to -0.3
- vir_energy: float32 [448], replicated, may hold values from 0.3 to 3
Outputs:
- gamma: float32 [8, 448, 1536], P('occ', None, 'aux')
The draws below stay inside these ranges and needn't reach their ends.
All inputs are finite; a program needn't handle non-finite values.
Results may differ from the reference program's by a relative error of at most 0.0019.
Values may be sent and summed in bfloat16 or wider, within the bound.
A program may use at most 64 MiB of HBM per device.

```python
import jax
import jax.numpy as jnp
from jax import lax

NVIR = 448
NOCC = 8
NAUX = 1536


def steps_of(rng, extent, cuts, least, top_value):
    level = 1.0
    for axis_at, parts in cuts:
        steps = jax.random.uniform(jax.random.fold_in(jax.random.fold_in(rng, 6), axis_at), (parts,), jnp.float32, least / len(cuts), top_value / len(cuts))
        level = level * jnp.repeat(jnp.exp(steps), extent[axis_at] // parts).reshape((-1,) + (1,) * (len(extent) - 1 - axis_at))
    return level


def noise(stream_key, dims, deviation, most, pieces=(), kind=jnp.bfloat16):
    result = deviation * jax.random.normal(stream_key, dims, jnp.float32)
    if pieces:
        result = result * steps_of(stream_key, dims, pieces, -0.22, 0.18)
    return jnp.clip(result, -most, most).astype(kind)


def setup_inputs(seed: int = 0) -> dict:
    key_of = jax.random.split(jax.random.key(seed), 4)
    return {
        "three_index": noise(key_of[0], (NOCC, NVIR, NAUX), 0.05, 0.75, ((0, 8), (2, 4))),
        "occ_energy": jnp.clip(-2.0 + 1.7 * jax.random.uniform(key_of[1], (NOCC,), jnp.float32) ** steps_of(key_of[1], (NOCC,), ((0, 8),), -0.2, 0.2), -2.0, -0.3),
        "vir_energy": jnp.clip(jax.random.uniform(key_of[2], (NVIR,), jnp.float32, 0.3, 3.0), 0.3, 3.0),
    }


def reference(three_index, occ_energy, vir_energy):
    rows = three_index.reshape(NOCC * NVIR, NAUX)
    pair = lax.dot_general(rows, rows, (((1,), (1,)), ((), ())), preferred_element_type=jnp.float32)
    four = pair.reshape(NOCC, NVIR, NOCC, NVIR)
    swapped = jnp.transpose(four, (0, 3, 2, 1))
    denom = (vir_energy[None, :, None, None] + vir_energy[None, None, None, :]
             - occ_energy[:, None, None, None] - occ_energy[None, None, :, None])
    amps = ((2.0 * four - swapped) / denom).astype(jnp.bfloat16).reshape(NOCC * NVIR, NOCC * NVIR)
    gamma = jnp.dot(amps, rows, preferred_element_type=jnp.float32)
    return gamma.reshape(NOCC, NVIR, NAUX)
```

```python
import functools
import heapq

import jax
import jax.numpy as jnp
from jax import lax
from jax.experimental import pallas as pl
from jax.experimental.pallas import tpu as pltpu
from jax.sharding import PartitionSpec as P

MESH = pl.DeviceIdType.MESH
CORES = 2
GATHER_LIMIT = 24 * 1024 * 1024
PIECES = ((0.5, "xyz"), (0.25, "zyx"), (0.25, "zxy"))
RATE = {"x": 46.0, "y": 46.0, "z": 46.0, "c": 150.0}
HOP = {"x": 1700.0, "y": 1700.0, "z": 1700.0, "c": 900.0}


def from_behind(array, axis, by):
    size = lax.axis_size(axis)
    return lax.ppermute(array, axis, [(i, (i + by) % size) for i in range(size)])


def reach(size):
    return {1: size // 2, -1: (size - 1) // 2}


def piece_rows(rows):
    pieces, low = [], 0
    for at, (share, order) in enumerate(PIECES):
        count = int(rows * share) // 16 * 16
        if at == len(PIECES) - 1:
            count = rows - low
        pieces.append((low, count, order))
        low += count
    return pieces


def moves(rel, arrived, order, sizes, flip):
    out = []
    first = 0
    if arrived is not None:
        way = 1 if rel[arrived] > 0 else -1
        if abs(rel[arrived]) < reach(sizes[arrived])[way]:
            out.append((arrived, way))
        first = order.index(arrived) + 1
    for dim in order[first:]:
        for way in (1, -1):
            if reach(sizes[dim])[way] >= 1:
                out.append((dim, way))
    return out


def plan(rows, width, sizes):
    pieces = piece_rows(rows)
    free = {}
    heap, count = [], 0
    for at, (_, _, order) in enumerate(pieces):
        heap.append((0.0, count, at, (0, 0, 0), None, "own"))
        count += 1
    heapq.heapify(heap)
    events = []

    def queue(link, now, size):
        start = max(now, free.get(link, 0.0))
        free[link] = start + size / RATE[link[0]]
        return free[link] + HOP[link[0]]

    while heap:
        now, _, at, rel, arrived, kind = heapq.heappop(heap)
        low, number, order = pieces[at]
        size = number * width * 2
        if kind == "core":
            events.append((now, at, rel, "core", ()))
            continue
        named = dict(zip("xyz", rel))
        onward = moves(named, arrived, order, sizes, None)
        sends = []
        for dim, way in onward:
            when = queue((dim, way), now, size)
            after = dict(named)
            after[dim] += way
            heapq.heappush(heap, (when, count, at, (after["x"], after["y"], after["z"]), dim, "link"))
            count += 1
            sends.append((dim, way))
        when = queue(("c", 1), now, size)
        heapq.heappush(heap, (when, count, at, rel, None, "core"))
        count += 1
        events.append((now, at, rel, kind, tuple(sends)))
    return pieces, events


def gather_kernel(nz, nx, ny, b_ref, e_ref, col_ref, row_ref, out_ref, blocks, energies,
                  send_sem, recv_sem, esend_sem, erecv_sem, own_sem):
    rows, width = b_ref.shape
    occ, aux = lax.axis_index("occ"), lax.axis_index("aux")
    z, x = occ // nx, occ % nx
    y, core = aux // CORES, aux % CORES
    sizes = {"x": nx, "y": ny, "z": nz}
    turn = 1 - 2 * core
    pieces, events = plan(rows, width, sizes)
    nocc = nz * nx

    def device(dx, dy, dz, dc):
        return (
            ((z + turn * dz + nz) % nz) * nx + (x + dx + nx) % nx,
            ((y + dy + ny) % ny) * CORES + (core + dc) % CORES,
        )

    barrier = pltpu.get_barrier_semaphore()
    for step in range(1, nocc):
        pl.semaphore_signal(barrier, inc=1, device_id=((occ + step) % nocc, aux), device_id_type=MESH)
    near = [(occ, (aux // CORES) * CORES + (core + 1) % CORES)]
    for way in (1, -1):
        if reach(ny)[way] >= 1:
            near.append(device(0, way, 0, 0))
    for target in near:
        pl.semaphore_signal(barrier, inc=1, device_id=target, device_id_type=MESH)
    pl.semaphore_wait(barrier, nocc - 1 + len(near))

    def columns(shard_aux):
        return pl.ds(pl.multiple_of(shard_aux * width, width), width)

    def place(at, shard):
        low, number, _ = pieces[at]
        return blocks.at[shard[0], pl.ds(low, number), columns(shard[1])]

    def source(at, shard, own):
        low, number, _ = pieces[at]
        return b_ref.at[pl.ds(low, number)] if own else place(at, shard)

    own_copy = pltpu.make_async_copy(b_ref, blocks.at[occ, :, columns(aux)], own_sem)
    own_copy.start()
    sent = []

    def send(at, shard, own, target):
        copy = pltpu.make_async_remote_copy(
            src_ref=source(at, shard, own), dst_ref=place(at, shard),
            send_sem=send_sem.at[len(sent)], recv_sem=recv_sem.at[at, shard[0], shard[1]],
            device_id=target, device_id_type=MESH,
        )
        copy.start()
        sent.append(copy)

    def arrive(at, shard):
        spot = place(at, shard)
        pltpu.make_async_remote_copy(
            src_ref=spot, dst_ref=spot, send_sem=own_sem, recv_sem=recv_sem.at[at, shard[0], shard[1]],
            device_id=(occ, aux), device_id_type=MESH,
        ).wait_recv()

    left = {}
    ready = []
    for _, at, rel, kind, _ in events:
        key = (rel[0] % nx, rel[2] % nz)
        left[key] = left.get(key, 0) + 1
    waiting = {"energies": True}
    small = []
    done = [False]

    def compute(key):
        block = device(-key[0], 0, -key[1], 0)[0]
        mine, other = blocks.at[occ], blocks.at[block]
        value = lax.dot_general(mine[...], other[...], (((1,), (1,)), ((), ())), preferred_element_type=jnp.float32)
        numer = 2.0 * value - value.T
        denom = col_ref[...] + row_ref[...] - e_ref[0:1, 0:1] - energies[block, 0:1, 0:1]
        amps = (numer / denom).astype(jnp.bfloat16)
        term = jnp.dot(amps, blocks[block, :, columns(aux)], preferred_element_type=jnp.float32)
        out_ref[...] = out_ref[...] + term if done[0] else term
        done[0] = True

    started = False
    for _, at, rel, kind, sends in events:
        dx, dy, dz = -rel[0], -rel[1], -rel[2]
        key = (rel[0] % nx, rel[2] % nz)
        if kind == "core":
            arrive(at, partner_shard(device, nz, nx, z, x, y, core, turn, dx, dy, dz, ny))
            rel_key = (rel[0] % nx, (-rel[2]) % nz)
            key = rel_key
        else:
            shard = device(dx, dy, dz, 0)
            if kind == "link":
                arrive(at, shard)
            for dim, way in sends:
                step = {"x": 0, "y": 0, "z": 0}
                step[dim] = way
                send(at, shard, kind == "own", device(step["x"], step["y"], step["z"], 0))
            send(at, shard, kind == "own", device(0, 0, 0, 1))
        left[key] -= 1
        if kind == "own" and not started and at == len(pieces) - 1:
            started = True
            keep = pltpu.make_async_copy(e_ref, energies.at[occ], esend_sem.at[0])
            keep.start()
            for step in range(1, nocc):
                copy = pltpu.make_async_remote_copy(
                    src_ref=e_ref, dst_ref=energies.at[occ], send_sem=esend_sem.at[step],
                    recv_sem=erecv_sem.at[occ], device_id=((occ + step) % nocc, aux), device_id_type=MESH,
                )
                copy.start()
                small.append(copy)
            keep.wait()
            own_copy.wait()
        if left[key] == 0:
            left[key] = -1
            ready.append(key)
            if (0, 0) in ready or done[0]:
                for one in ready:
                    if one != (0, 0) and waiting["energies"]:
                        waiting["energies"] = False
                        for step in range(1, nocc):
                            who = (occ + step) % nocc
                            pltpu.make_async_remote_copy(
                                src_ref=e_ref, dst_ref=energies.at[who], send_sem=own_sem,
                                recv_sem=erecv_sem.at[who], device_id=(occ, aux), device_id_type=MESH,
                            ).wait_recv()
                    compute(one)
                ready.clear()
    for copy in sent + small:
        copy.wait_send()


def partner_shard(device, nz, nx, z, x, y, core, turn, dx, dy, dz, ny):
    return (
        ((z - turn * dz + nz) % nz) * nx + (x + dx + nx) % nx,
        ((y + dy + ny) % ny) * CORES + (core + 1) % CORES,
    )


def gathered(three_index, occ_energy, vir_energy, nz, nx, ny):
    _, rows, width = three_index.shape
    nocc, naux = nz * nx, ny * CORES
    pieces, events = plan(rows, width, {"x": nx, "y": ny, "z": nz})
    copies = sum(len(e[4]) + 1 for e in events if e[3] != "core")
    energy = jnp.broadcast_to(occ_energy.reshape(1, 1), (8, 128))
    vmem = pl.BlockSpec(memory_space=pltpu.VMEM)
    out = pl.pallas_call(
        functools.partial(gather_kernel, nz, nx, ny),
        out_shape=jax.ShapeDtypeStruct((rows, width), jnp.float32),
        in_specs=[vmem] * 4,
        out_specs=vmem,
        scratch_shapes=[
            pltpu.VMEM((nocc, rows, naux * width), three_index.dtype),
            pltpu.VMEM((nocc, 8, 128), jnp.float32),
            pltpu.SemaphoreType.DMA((copies,)),
            pltpu.SemaphoreType.DMA((len(pieces), nocc, naux)),
            pltpu.SemaphoreType.DMA((nocc,)),
            pltpu.SemaphoreType.DMA((nocc,)),
            pltpu.SemaphoreType.DMA,
        ],
        compiler_params=pltpu.CompilerParams(
            collective_id=0, has_side_effects=True, vmem_limit_bytes=48 * 1024 * 1024
        ),
    )(three_index[0], energy, vir_energy[:, None], vir_energy[None, :])
    return out[None]


def pair_amps(rows_i, eps_i, rows_j, eps_j, vir_energy):
    partial_value = lax.dot_general(
        rows_i, rows_j, (((1,), (1,)), ((), ())), preferred_element_type=jnp.float32
    )
    occ_count = eps_i.shape[0]
    vir_count = vir_energy.shape[0]
    width = occ_count * vir_count
    four = partial_value.reshape(occ_count, vir_count, occ_count, vir_count)
    numer = (2.0 * four - jnp.transpose(four, (0, 3, 2, 1))).reshape(width, width)
    denom = (
        vir_energy[None, :, None, None]
        + vir_energy[None, None, None, :]
        - eps_i[:, None, None, None]
        - eps_j[None, None, :, None]
    ).reshape(width, width)
    share = width // lax.axis_size("aux")
    mine = lax.psum_scatter(numer, "aux", scatter_dimension=0, tiled=True)
    lower = lax.axis_index("aux") * share
    denom_rows = lax.dynamic_slice_in_dim(denom, lower, share, 0)
    amps_rows = (mine / denom_rows).astype(jnp.bfloat16)
    amps = lax.all_gather(amps_rows, "aux", axis=0, tiled=True)
    return amps


def apply_other(amps, rows_i):
    return lax.dot_general(
        amps, rows_i, (((0,), (0,)), ((), ())), preferred_element_type=jnp.float32
    )


def local(three_index, occ_energy, vir_energy):
    occ_count, vir_count, aux_count = three_index.shape
    cycle_size = lax.axis_size("occ")
    my_index = lax.axis_index("occ")
    all_energy = lax.all_gather(occ_energy, "occ", axis=0, tiled=True)
    own_rows = three_index.reshape(occ_count * vir_count, aux_count)

    def energy_of(step):
        block = (my_index - step + cycle_size) % cycle_size
        return lax.dynamic_slice_in_dim(all_energy, block * occ_count, occ_count)

    amps = pair_amps(own_rows, occ_energy, own_rows, occ_energy, vir_energy)
    gamma = jnp.dot(amps, own_rows, preferred_element_type=jnp.float32)
    half = cycle_size // 2
    carried = jnp.zeros_like(gamma)

    def cycle_step(step, state):
        rows_j, carried, gamma = state
        rows_j = from_behind(rows_j, "occ", 1)
        carried = from_behind(carried, "occ", 1)
        amps = pair_amps(own_rows, occ_energy, rows_j, energy_of(step), vir_energy)
        gamma = gamma + jnp.dot(amps, rows_j, preferred_element_type=jnp.float32)
        carried = carried + apply_other(amps, own_rows)
        return (rows_j, carried, gamma)

    rows_j, carried, gamma = lax.fori_loop(1, half, cycle_step, (own_rows, carried, gamma))
    rows_j = from_behind(rows_j, "occ", 1)
    amps = pair_amps(own_rows, occ_energy, rows_j, energy_of(half), vir_energy)
    gamma = gamma + jnp.dot(amps, rows_j, preferred_element_type=jnp.float32)
    returned = from_behind(carried, "occ", 1 - half)
    gamma = gamma + returned
    return gamma.reshape(occ_count, vir_count, aux_count)


def solution(mesh):
    nocc, naux = mesh.shape["occ"], mesh.shape["aux"]

    def either(three_index, occ_energy, vir_energy):
        _, rows, width = three_index.shape
        whole = nocc * naux * three_index.size * three_index.dtype.itemsize
        fits = whole <= GATHER_LIMIT and three_index.shape[0] == 1
        if fits and naux % CORES == 0 and nocc % 2 == 0:
            return gathered(three_index, occ_energy, vir_energy, nocc // 2, 2, naux // CORES)
        return local(three_index, occ_energy, vir_energy)

    return jax.shard_map(
        either,
        mesh=mesh,
        in_specs=(P("occ", None, "aux"), P("occ"), P()),
        out_specs=P("occ", None, "aux"),
        check_vma=False,
    )
```

```python
import functools
import heapq
import itertools

import jax
import jax.numpy as jnp
from jax import lax
from jax.experimental import pallas as pl
from jax.experimental.pallas import tpu as pltpu
from jax.sharding import PartitionSpec as P

MESH = pl.DeviceIdType.MESH
CORES = 2
GATHER_LIMIT = 24 * 1024 * 1024
PIECES = ((0.393, "zyx"), (0.393, "zxy"), (0.214, "xyz"))
RATE = 90.0
HOP = 1650.0
ROUNDS = 6


def from_behind(array, axis, by):
    size = lax.axis_size(axis)
    return lax.ppermute(array, axis, [(i, (i + by) % size) for i in range(size)])


def piece_rows(rows):
    pieces, low = [], 0
    for at, (share, order) in enumerate(PIECES):
        last = at == len(PIECES) - 1
        count = rows - low if last else int(rows * share) // 16 * 16
        pieces.append((low, count, order))
        low += count
    return pieces


def onward(order, event, sizes):
    _, dx, dy, dz = event
    came = {"x": dx, "y": dy, "z": dz}
    moved = [dim for dim in order if came[dim] != 0]
    pairs, first = [], 0
    if moved:
        first = order.index(moved[-1]) + 1
        if moved[-1] == "z":
            pairs.append(("z", -1 if dz > 0 else 1))
    for dim in order[first:]:
        if sizes[dim] > 1:
            pairs.extend([("z", 1), ("z", -1)] if dim == "z" else [(dim, 1)])
    return pairs


def timed(pieces, events, sizes, row_bytes):
    nx, ny, nz = sizes["x"], sizes["y"], sizes["z"]
    chips = list(itertools.product(range(nz), range(nx), range(ny)))

    def home(chip, event):
        return (chip[0] + event[3], (chip[1] + event[1]) % nx, (chip[2] + event[2]) % ny)

    def beside(chip, dim, way):
        z, x, y = chip
        return {"z": (z + way, x, y), "x": (z, (x + way) % nx, y), "y": (z, x, (y + way) % ny)}[dim]

    todo = {c: [e for e in events if 0 <= c[0] + e[3] < nz] for c in chips}
    at_place = {c: 0 for c in chips}
    arrived = {c: {} for c in chips}
    free, heap, ticket = {}, [], itertools.count()

    def advance(chip, now):
        while at_place[chip] < len(todo[chip]):
            event = todo[chip][at_place[chip]]
            key = (event[0], home(chip, event))
            if key[1] != chip and key not in arrived[chip]:
                return
            at_place[chip] += 1
            _, count, order = pieces[event[0]]
            for dim, way in onward(order, event, sizes):
                target = beside(chip, dim, way)
                if 0 <= target[0] < nz:
                    sent = max(now, free.get((chip, target), 0.0)) + CORES * count * row_bytes / RATE
                    free[chip, target] = sent
                    heapq.heappush(heap, (sent + HOP, next(ticket), target, key))

    for chip in chips:
        advance(chip, 0.0)
    end = 0.0
    while heap:
        end, _, chip, key = heapq.heappop(heap)
        arrived[chip][key] = end
        advance(chip, end)
    times = []
    for event in events:
        seen = [arrived[c].get((event[0], home(c, event)), 0.0) for c in chips if 0 <= c[0] + event[3] < nz]
        times.append((sum(seen) / len(seen) + max(seen)) / 2)
    return end, times


def plan(rows, width, sizes):
    pieces = piece_rows(rows)
    span = range(1 - sizes["z"], sizes["z"])
    events = [
        (at, dx, dy, dz)
        for at in range(len(pieces)) for dz in span
        for dx in range(sizes["x"]) for dy in range(sizes["y"])
    ]
    events.sort(key=lambda e: (e[1] + e[2] + abs(e[3]), e[0]))
    best = None
    for _ in range(ROUNDS):
        end, times = timed(pieces, events, sizes, width * 2)
        if best is None or end < best[0]:
            best = (end, list(events))
        order = sorted(range(len(events)), key=lambda k: times[k])
        events = [events[k] for k in order]
    return pieces, best[1]


def gather_kernel(nz, nx, ny, b_ref, e_ref, col_ref, row_ref, out_ref, blocks, energies,
                  send_sem, recv_sem, esend_sem, erecv_sem, own_sem):
    rows, width = b_ref.shape
    occ, aux = lax.axis_index("occ"), lax.axis_index("aux")
    z, x = occ // nx, occ % nx
    y, core = aux // CORES, aux % CORES
    sizes = {"x": nx, "y": ny, "z": nz}
    pieces, events = plan(rows, width, sizes)
    nocc = nz * nx

    def device(dx, dy, dz, dc):
        return ((z + dz) * nx + lax.rem(x + dx, nx), lax.rem(y + dy, ny) * CORES + lax.rem(core + dc, CORES))

    def inside(dz):
        return jnp.logical_and(z + dz >= 0, z + dz < nz)

    def when(dz, body):
        if dz == 0:
            body()
        else:
            pl.when(inside(dz))(body)

    barrier = pltpu.get_barrier_semaphore()
    peers = [((occ + step) % nocc, aux) for step in range(1, nocc)]
    near = peers + [device(0, 0, 0, 1)] + ([device(0, 1, 0, 0)] if ny > 1 else [])
    for target in near:
        pl.semaphore_signal(barrier, inc=1, device_id=target, device_id_type=MESH)

    def columns(shard_aux):
        return pl.ds(pl.multiple_of(shard_aux * width, width), width)

    own_copy = pltpu.make_async_copy(b_ref, blocks.at[occ, :, columns(aux)], own_sem)
    own_copy.start()
    keep = pltpu.make_async_copy(e_ref, energies.at[occ], esend_sem.at[0])
    keep.start()
    out_ref[...] = jnp.zeros_like(out_ref)
    pl.semaphore_wait(barrier, len(near))

    def place(at, shard):
        low, number, _ = pieces[at]
        return blocks.at[shard[0], pl.ds(low, number), columns(shard[1])]

    ends = []

    def send(at, event, shard, target, reached):
        low, number, _ = pieces[at]
        own = event[1:] == (0, 0, 0)
        slot = len(ends)

        def copy():
            return pltpu.make_async_remote_copy(
                src_ref=b_ref.at[pl.ds(low, number)] if own else place(at, shard),
                dst_ref=place(at, shard), send_sem=send_sem.at[slot],
                recv_sem=recv_sem.at[at, shard[0], shard[1]], device_id=target, device_id_type=MESH,
            )

        when(reached, lambda: copy().start())
        ends.append((event[3], reached, lambda: copy().wait_send()))

    def arrive(at, shard):
        spot = place(at, shard)
        pltpu.make_async_remote_copy(
            src_ref=spot, dst_ref=spot, send_sem=own_sem, recv_sem=recv_sem.at[at, shard[0], shard[1]],
            device_id=(occ, aux), device_id_type=MESH,
        ).wait_recv()

    def compute(dx, dz):
        block = device(dx, 0, dz, 0)[0]
        for at in range(len(pieces)):
            for dy in range(ny):
                arrive(at, device(dx, dy, dz, 1))
        value = lax.dot_general(
            blocks[occ], blocks[block], (((1,), (1,)), ((), ())), preferred_element_type=jnp.float32
        )
        numer = 2.0 * value - value.T
        denom = col_ref[...] + row_ref[...] - e_ref[0:1, 0:1] - energies[block, 0:1, 0:1]
        amps = (numer / denom).astype(jnp.bfloat16)
        out_ref[...] += jnp.dot(amps, blocks[block, :, columns(aux)], preferred_element_type=jnp.float32)

    left = {}
    for event in events:
        left[event[1], event[3]] = left.get((event[1], event[3]), 0) + 1
    full, small, held = False, [], []
    for event in events:
        at, dx, dy, dz = event
        shard = device(dx, dy, dz, 0)

        steps = [{"x": 0, "y": 0, "z": 0, dim: way} for dim, way in onward(pieces[at][2], event, sizes)]
        targets = [(device(o["x"], o["y"], o["z"], 0), o["z"]) for o in steps] + [(device(0, 0, 0, 1), 0)]

        def pass_on(at=at, event=event, shard=shard, targets=targets):
            if event[1:] != (0, 0, 0):
                arrive(at, shard)
            for target, reached in targets:
                send(at, event, shard, target, reached)

        when(dz, pass_on)
        left[dx, dz] -= 1
        if left[dx, dz] == 0:
            held.append((dx, dz))
        if (0, 0) in held and not full:
            full = True
            for step, target in enumerate(peers, 1):
                copy = pltpu.make_async_remote_copy(
                    src_ref=e_ref, dst_ref=energies.at[occ], send_sem=esend_sem.at[step],
                    recv_sem=erecv_sem.at[occ], device_id=target, device_id_type=MESH,
                )
                copy.start()
                small.append(copy)
            keep.wait()
            own_copy.wait()
            for who, _ in peers:
                pltpu.make_async_remote_copy(
                    src_ref=e_ref, dst_ref=energies.at[who], send_sem=own_sem,
                    recv_sem=erecv_sem.at[who], device_id=(occ, aux), device_id_type=MESH,
                ).wait_recv()
        if full:
            for one in held:
                when(one[1], functools.partial(compute, *one))
            held = []
    for copy in small:
        copy.wait_send()
    for came, reached, wait in ends:
        when(came, functools.partial(when, reached, wait))


def gathered(three_index, occ_energy, vir_energy, nz, nx, ny):
    _, rows, width = three_index.shape
    nocc, naux = nz * nx, ny * CORES
    sizes = {"x": nx, "y": ny, "z": nz}
    pieces, events = plan(rows, width, sizes)
    copies = sum(len(onward(pieces[e[0]][2], e, sizes)) + 1 for e in events)
    energy = jnp.broadcast_to(occ_energy.reshape(1, 1), (8, 128))
    vmem = pl.BlockSpec(memory_space=pltpu.VMEM)
    out = pl.pallas_call(
        functools.partial(gather_kernel, nz, nx, ny),
        out_shape=jax.ShapeDtypeStruct((rows, width), jnp.float32),
        in_specs=[vmem] * 4,
        out_specs=vmem,
        scratch_shapes=[
            pltpu.VMEM((nocc, rows, naux * width), three_index.dtype),
            pltpu.VMEM((nocc, 8, 128), jnp.float32),
            pltpu.SemaphoreType.DMA((copies,)),
            pltpu.SemaphoreType.DMA((len(pieces), nocc, naux)),
            pltpu.SemaphoreType.DMA((nocc,)),
            pltpu.SemaphoreType.DMA((nocc,)),
            pltpu.SemaphoreType.DMA,
        ],
        compiler_params=pltpu.CompilerParams(
            collective_id=0, has_side_effects=True, vmem_limit_bytes=48 * 1024 * 1024
        ),
    )(three_index[0], energy, vir_energy[:, None], vir_energy[None, :])
    return out[None]


def pair_amps(rows_i, eps_i, rows_j, eps_j, vir_energy):
    partial_value = lax.dot_general(
        rows_i, rows_j, (((1,), (1,)), ((), ())), preferred_element_type=jnp.float32
    )
    occ_count = eps_i.shape[0]
    vir_count = vir_energy.shape[0]
    width = occ_count * vir_count
    four = partial_value.reshape(occ_count, vir_count, occ_count, vir_count)
    numer = (2.0 * four - jnp.transpose(four, (0, 3, 2, 1))).reshape(width, width)
    denom = (
        vir_energy[None, :, None, None]
        + vir_energy[None, None, None, :]
        - eps_i[:, None, None, None]
        - eps_j[None, None, :, None]
    ).reshape(width, width)
    share = width // lax.axis_size("aux")
    mine = lax.psum_scatter(numer, "aux", scatter_dimension=0, tiled=True)
    lower = lax.axis_index("aux") * share
    denom_rows = lax.dynamic_slice_in_dim(denom, lower, share, 0)
    amps_rows = (mine / denom_rows).astype(jnp.bfloat16)
    amps = lax.all_gather(amps_rows, "aux", axis=0, tiled=True)
    return amps


def apply_other(amps, rows_i):
    return lax.dot_general(
        amps, rows_i, (((0,), (0,)), ((), ())), preferred_element_type=jnp.float32
    )


def local(three_index, occ_energy, vir_energy):
    occ_count, vir_count, aux_count = three_index.shape
    cycle_size = lax.axis_size("occ")
    my_index = lax.axis_index("occ")
    all_energy = lax.all_gather(occ_energy, "occ", axis=0, tiled=True)
    own_rows = three_index.reshape(occ_count * vir_count, aux_count)

    def energy_of(step):
        block = (my_index - step + cycle_size) % cycle_size
        return lax.dynamic_slice_in_dim(all_energy, block * occ_count, occ_count)

    amps = pair_amps(own_rows, occ_energy, own_rows, occ_energy, vir_energy)
    gamma = jnp.dot(amps, own_rows, preferred_element_type=jnp.float32)
    half = cycle_size // 2
    carried = jnp.zeros_like(gamma)

    def cycle_step(step, state):
        rows_j, carried, gamma = state
        rows_j = from_behind(rows_j, "occ", 1)
        carried = from_behind(carried, "occ", 1)
        amps = pair_amps(own_rows, occ_energy, rows_j, energy_of(step), vir_energy)
        gamma = gamma + jnp.dot(amps, rows_j, preferred_element_type=jnp.float32)
        carried = carried + apply_other(amps, own_rows)
        return (rows_j, carried, gamma)

    rows_j, carried, gamma = lax.fori_loop(1, half, cycle_step, (own_rows, carried, gamma))
    rows_j = from_behind(rows_j, "occ", 1)
    amps = pair_amps(own_rows, occ_energy, rows_j, energy_of(half), vir_energy)
    gamma = gamma + jnp.dot(amps, rows_j, preferred_element_type=jnp.float32)
    returned = from_behind(carried, "occ", 1 - half)
    gamma = gamma + returned
    return gamma.reshape(occ_count, vir_count, aux_count)


def solution(mesh):
    nocc, naux = mesh.shape["occ"], mesh.shape["aux"]
    pairs = 2 if nocc % 2 == 0 else 1

    def either(three_index, occ_energy, vir_energy):
        held, rows, width = three_index.shape
        whole = nocc * naux * three_index.size * three_index.dtype.itemsize
        even = held == 1 and rows % 16 == 0 and width % 128 == 0
        if whole <= GATHER_LIMIT and even and naux in (CORES, 2 * CORES):
            return gathered(three_index, occ_energy, vir_energy, nocc // pairs, pairs, naux // CORES)
        return local(three_index, occ_energy, vir_energy)

    return jax.shard_map(
        either,
        mesh=mesh,
        in_specs=(P("occ", None, "aux"), P("occ"), P()),
        out_specs=P("occ", None, "aux"),
        check_vma=False,
    )
```

```python
import functools
import heapq

import jax
import jax.numpy as jnp
from jax import lax
from jax.experimental import pallas as pl
from jax.experimental.pallas import tpu as pltpu
from jax.sharding import PartitionSpec as P

MESH = pl.DeviceIdType.MESH
CORES = 2
GATHER_LIMIT = 24 * 1024 * 1024
PIECES = ((0.145, "yxz"), (0.43, "zyx"), (0.43, "zxy"))
RATE = {"x": 46.0, "y": 46.0, "z": 25.0, "c": 150.0}
HOP = {"x": 1700.0, "y": 1700.0, "z": 1700.0, "c": 900.0}


def from_behind(array, axis, by):
    size = lax.axis_size(axis)
    return lax.ppermute(array, axis, [(i, (i + by) % size) for i in range(size)])


def reach(size):
    return {1: size // 2, -1: (size - 1) // 2}


def piece_rows(rows):
    pieces, low = [], 0
    for at, (share, order) in enumerate(PIECES):
        count = int(rows * share) // 16 * 16
        if at == len(PIECES) - 1:
            count = rows - low
        pieces.append((low, count, order))
        low += count
    return pieces


def moves(rel, arrived, order, sizes, flip):
    out = []
    first = 0
    if arrived is not None:
        way = 1 if rel[arrived] > 0 else -1
        if abs(rel[arrived]) < reach(sizes[arrived])[way]:
            out.append((arrived, way))
        first = order.index(arrived) + 1
    for dim in order[first:]:
        for way in (1, -1):
            if reach(sizes[dim])[way] >= 1:
                out.append((dim, way))
    return out


def plan(rows, width, sizes):
    pieces = piece_rows(rows)
    free = {}
    heap, count = [], 0
    for at, (_, _, order) in enumerate(pieces):
        heap.append((0.0, count, at, (0, 0, 0), None, "own"))
        count += 1
    heapq.heapify(heap)
    events = []

    def queue(link, now, size):
        start = max(now, free.get(link, 0.0))
        free[link] = start + size / RATE[link[0]]
        return free[link] + HOP[link[0]]

    while heap:
        now, _, at, rel, arrived, kind = heapq.heappop(heap)
        low, number, order = pieces[at]
        size = number * width * 2
        if kind == "core":
            events.append((now, at, rel, "core", ()))
            continue
        named = dict(zip("xyz", rel))
        onward = moves(named, arrived, order, sizes, None)
        sends = []
        for dim, way in onward:
            when = queue((dim, way), now, size)
            after = dict(named)
            after[dim] += way
            heapq.heappush(heap, (when, count, at, (after["x"], after["y"], after["z"]), dim, "link"))
            count += 1
            sends.append((dim, way))
        when = queue(("c", 1), now, size)
        heapq.heappush(heap, (when, count, at, rel, None, "core"))
        count += 1
        events.append((now, at, rel, kind, tuple(sends)))
    return pieces, events


def gather_kernel(nz, nx, ny, b_ref, e_ref, col_ref, row_ref, out_ref, blocks, energies,
                  send_sem, recv_sem, esend_sem, erecv_sem, own_sem):
    rows, width = b_ref.shape
    occ, aux = lax.axis_index("occ"), lax.axis_index("aux")
    z, x = occ // nx, occ % nx
    y, core = aux // CORES, aux % CORES
    sizes = {"x": nx, "y": ny, "z": nz}
    turn = 1 - 2 * core
    pieces, events = plan(rows, width, sizes)
    nocc = nz * nx

    def device(dx, dy, dz, dc):
        return (
            ((z + turn * dz + nz) % nz) * nx + (x + dx + nx) % nx,
            ((y + dy + ny) % ny) * CORES + (core + dc) % CORES,
        )

    barrier = pltpu.get_barrier_semaphore()
    for step in range(1, nocc):
        pl.semaphore_signal(barrier, inc=1, device_id=((occ + step) % nocc, aux), device_id_type=MESH)
    near = [(occ, (aux // CORES) * CORES + (core + 1) % CORES)]
    for way in (1, -1):
        if reach(ny)[way] >= 1:
            near.append(device(0, way, 0, 0))
    for target in near:
        pl.semaphore_signal(barrier, inc=1, device_id=target, device_id_type=MESH)
    pl.semaphore_wait(barrier, nocc - 1 + len(near))

    def columns(shard_aux):
        return pl.ds(pl.multiple_of(shard_aux * width, width), width)

    def place(at, shard):
        low, number, _ = pieces[at]
        return blocks.at[shard[0], pl.ds(low, number), columns(shard[1])]

    def source(at, shard, own):
        low, number, _ = pieces[at]
        return b_ref.at[pl.ds(low, number)] if own else place(at, shard)

    own_copy = pltpu.make_async_copy(b_ref, blocks.at[occ, :, columns(aux)], own_sem)
    own_copy.start()
    sent = []

    def send(at, shard, own, target):
        copy = pltpu.make_async_remote_copy(
            src_ref=source(at, shard, own), dst_ref=place(at, shard),
            send_sem=send_sem.at[len(sent)], recv_sem=recv_sem.at[at, shard[0], shard[1]],
            device_id=target, device_id_type=MESH,
        )
        copy.start()
        sent.append(copy)

    def arrive(at, shard):
        spot = place(at, shard)
        pltpu.make_async_remote_copy(
            src_ref=spot, dst_ref=spot, send_sem=own_sem, recv_sem=recv_sem.at[at, shard[0], shard[1]],
            device_id=(occ, aux), device_id_type=MESH,
        ).wait_recv()

    left = {}
    ready = []
    for _, at, rel, kind, _ in events:
        key = (rel[0] % nx, rel[2] % nz)
        left[key] = left.get(key, 0) + 1
    waiting = {"energies": True}
    small = []
    done = [False]

    def compute(key):
        block = device(-key[0], 0, -key[1], 0)[0]
        mine, other = blocks.at[occ], blocks.at[block]
        value = lax.dot_general(mine[...], other[...], (((1,), (1,)), ((), ())), preferred_element_type=jnp.float32)
        numer = 2.0 * value - value.T
        denom = col_ref[...] + row_ref[...] - e_ref[0:1, 0:1] - energies[block, 0:1, 0:1]
        amps = (numer / denom).astype(jnp.bfloat16)
        term = jnp.dot(amps, blocks[block, :, columns(aux)], preferred_element_type=jnp.float32)
        out_ref[...] = out_ref[...] + term if done[0] else term
        done[0] = True

    started = False
    for _, at, rel, kind, sends in events:
        dx, dy, dz = -rel[0], -rel[1], -rel[2]
        key = (rel[0] % nx, rel[2] % nz)
        if kind == "core":
            arrive(at, partner_shard(device, nz, nx, z, x, y, core, turn, dx, dy, dz, ny))
            rel_key = (rel[0] % nx, (-rel[2]) % nz)
            key = rel_key
        else:
            shard = device(dx, dy, dz, 0)
            if kind == "link":
                arrive(at, shard)
            for dim, way in sends:
                step = {"x": 0, "y": 0, "z": 0}
                step[dim] = way
                send(at, shard, kind == "own", device(step["x"], step["y"], step["z"], 0))
            send(at, shard, kind == "own", device(0, 0, 0, 1))
        left[key] -= 1
        if kind == "own" and not started and at == len(pieces) - 1:
            started = True
            keep = pltpu.make_async_copy(e_ref, energies.at[occ], esend_sem.at[0])
            keep.start()
            for step in range(1, nocc):
                copy = pltpu.make_async_remote_copy(
                    src_ref=e_ref, dst_ref=energies.at[occ], send_sem=esend_sem.at[step],
                    recv_sem=erecv_sem.at[occ], device_id=((occ + step) % nocc, aux), device_id_type=MESH,
                )
                copy.start()
                small.append(copy)
            keep.wait()
            own_copy.wait()
        if left[key] == 0:
            left[key] = -1
            ready.append(key)
            if (0, 0) in ready or done[0]:
                for one in ready:
                    if one != (0, 0) and waiting["energies"]:
                        waiting["energies"] = False
                        for step in range(1, nocc):
                            who = (occ + step) % nocc
                            pltpu.make_async_remote_copy(
                                src_ref=e_ref, dst_ref=energies.at[who], send_sem=own_sem,
                                recv_sem=erecv_sem.at[who], device_id=(occ, aux), device_id_type=MESH,
                            ).wait_recv()
                    compute(one)
                ready.clear()
    for copy in sent + small:
        copy.wait_send()


def partner_shard(device, nz, nx, z, x, y, core, turn, dx, dy, dz, ny):
    return (
        ((z - turn * dz + nz) % nz) * nx + (x + dx + nx) % nx,
        ((y + dy + ny) % ny) * CORES + (core + 1) % CORES,
    )


def gathered(three_index, occ_energy, vir_energy, nz, nx, ny):
    _, rows, width = three_index.shape
    nocc, naux = nz * nx, ny * CORES
    pieces, events = plan(rows, width, {"x": nx, "y": ny, "z": nz})
    copies = sum(len(e[4]) + 1 for e in events if e[3] != "core")
    energy = jnp.broadcast_to(occ_energy.reshape(1, 1), (8, 128))
    vmem = pl.BlockSpec(memory_space=pltpu.VMEM)
    out = pl.pallas_call(
        functools.partial(gather_kernel, nz, nx, ny),
        out_shape=jax.ShapeDtypeStruct((rows, width), jnp.float32),
        in_specs=[vmem] * 4,
        out_specs=vmem,
        scratch_shapes=[
            pltpu.VMEM((nocc, rows, naux * width), three_index.dtype),
            pltpu.VMEM((nocc, 8, 128), jnp.float32),
            pltpu.SemaphoreType.DMA((copies,)),
            pltpu.SemaphoreType.DMA((len(pieces), nocc, naux)),
            pltpu.SemaphoreType.DMA((nocc,)),
            pltpu.SemaphoreType.DMA((nocc,)),
            pltpu.SemaphoreType.DMA,
        ],
        compiler_params=pltpu.CompilerParams(
            collective_id=0, has_side_effects=True, vmem_limit_bytes=48 * 1024 * 1024
        ),
    )(three_index[0], energy, vir_energy[:, None], vir_energy[None, :])
    return out[None]


def pair_amps(rows_i, eps_i, rows_j, eps_j, vir_energy):
    partial_value = lax.dot_general(
        rows_i, rows_j, (((1,), (1,)), ((), ())), preferred_element_type=jnp.float32
    )
    occ_count = eps_i.shape[0]
    vir_count = vir_energy.shape[0]
    width = occ_count * vir_count
    four = partial_value.reshape(occ_count, vir_count, occ_count, vir_count)
    numer = (2.0 * four - jnp.transpose(four, (0, 3, 2, 1))).reshape(width, width)
    denom = (
        vir_energy[None, :, None, None]
        + vir_energy[None, None, None, :]
        - eps_i[:, None, None, None]
        - eps_j[None, None, :, None]
    ).reshape(width, width)
    share = width // lax.axis_size("aux")
    mine = lax.psum_scatter(numer, "aux", scatter_dimension=0, tiled=True)
    lower = lax.axis_index("aux") * share
    denom_rows = lax.dynamic_slice_in_dim(denom, lower, share, 0)
    amps_rows = (mine / denom_rows).astype(jnp.bfloat16)
    amps = lax.all_gather(amps_rows, "aux", axis=0, tiled=True)
    return amps


def apply_other(amps, rows_i):
    return lax.dot_general(
        amps, rows_i, (((0,), (0,)), ((), ())), preferred_element_type=jnp.float32
    )


def local(three_index, occ_energy, vir_energy):
    occ_count, vir_count, aux_count = three_index.shape
    cycle_size = lax.axis_size("occ")
    my_index = lax.axis_index("occ")
    all_energy = lax.all_gather(occ_energy, "occ", axis=0, tiled=True)
    own_rows = three_index.reshape(occ_count * vir_count, aux_count)

    def energy_of(step):
        block = (my_index - step + cycle_size) % cycle_size
        return lax.dynamic_slice_in_dim(all_energy, block * occ_count, occ_count)

    amps = pair_amps(own_rows, occ_energy, own_rows, occ_energy, vir_energy)
    gamma = jnp.dot(amps, own_rows, preferred_element_type=jnp.float32)
    half = cycle_size // 2
    carried = jnp.zeros_like(gamma)

    def cycle_step(step, state):
        rows_j, carried, gamma = state
        rows_j = from_behind(rows_j, "occ", 1)
        carried = from_behind(carried, "occ", 1)
        amps = pair_amps(own_rows, occ_energy, rows_j, energy_of(step), vir_energy)
        gamma = gamma + jnp.dot(amps, rows_j, preferred_element_type=jnp.float32)
        carried = carried + apply_other(amps, own_rows)
        return (rows_j, carried, gamma)

    rows_j, carried, gamma = lax.fori_loop(1, half, cycle_step, (own_rows, carried, gamma))
    rows_j = from_behind(rows_j, "occ", 1)
    amps = pair_amps(own_rows, occ_energy, rows_j, energy_of(half), vir_energy)
    gamma = gamma + jnp.dot(amps, rows_j, preferred_element_type=jnp.float32)
    returned = from_behind(carried, "occ", 1 - half)
    gamma = gamma + returned
    return gamma.reshape(occ_count, vir_count, aux_count)


def solution(mesh):
    nocc, naux = mesh.shape["occ"], mesh.shape["aux"]

    def either(three_index, occ_energy, vir_energy):
        _, rows, width = three_index.shape
        whole = nocc * naux * three_index.size * three_index.dtype.itemsize
        fits = whole <= GATHER_LIMIT and three_index.shape[0] == 1
        if fits and naux % CORES == 0 and nocc % 2 == 0:
            return gathered(three_index, occ_energy, vir_energy, nocc // 2, 2, naux // CORES)
        return local(three_index, occ_energy, vir_energy)

    return jax.shard_map(
        either,
        mesh=mesh,
        in_specs=(P("occ", None, "aux"), P("occ"), P()),
        out_specs=P("occ", None, "aux"),
        check_vma=False,
    )
```

```python
import functools
import heapq

import jax
import jax.numpy as jnp
from jax import lax
from jax.experimental import pallas as pl
from jax.experimental.pallas import tpu as pltpu
from jax.sharding import PartitionSpec as P

MESH = pl.DeviceIdType.MESH
CORES = 2
GATHER_LIMIT = 24 * 1024 * 1024
PIECES = ((0.11, "xyz"), (0.445, "zyx"), (0.445, "zxy"))
RATE = {"x": 46.0, "y": 46.0, "z": 25.0, "c": 150.0}
HOP = {"x": 1700.0, "y": 1700.0, "z": 3500.0, "c": 900.0}


def from_behind(array, axis, by):
    size = lax.axis_size(axis)
    return lax.ppermute(array, axis, [(i, (i + by) % size) for i in range(size)])


def reach(size):
    return {1: size // 2, -1: (size - 1) // 2}


def piece_rows(rows):
    pieces, low = [], 0
    for at, (share, order) in enumerate(PIECES):
        count = int(rows * share) // 16 * 16
        if at == len(PIECES) - 1:
            count = rows - low
        pieces.append((low, count, order))
        low += count
    return pieces


def moves(rel, arrived, order, sizes, flip):
    out = []
    first = 0
    if arrived is not None:
        way = 1 if rel[arrived] > 0 else -1
        if abs(rel[arrived]) < reach(sizes[arrived])[way]:
            out.append((arrived, way))
        first = order.index(arrived) + 1
    for dim in order[first:]:
        for way in (1, -1):
            if reach(sizes[dim])[way] >= 1:
                out.append((dim, way))
    return out


def plan(rows, width, sizes):
    pieces = piece_rows(rows)
    free = {}
    heap, count = [], 0
    for at, (_, _, order) in enumerate(pieces):
        heap.append((0.0, count, at, (0, 0, 0), None, "own"))
        count += 1
    heapq.heapify(heap)
    events = []

    def queue(link, now, size):
        start = max(now, free.get(link, 0.0))
        free[link] = start + size / RATE[link[0]]
        return free[link] + HOP[link[0]]

    while heap:
        now, _, at, rel, arrived, kind = heapq.heappop(heap)
        low, number, order = pieces[at]
        size = number * width * 2
        if kind == "core":
            events.append((now, at, rel, "core", ()))
            continue
        named = dict(zip("xyz", rel))
        onward = moves(named, arrived, order, sizes, None)
        sends = []
        for dim, way in onward:
            when = queue((dim, way), now, size)
            after = dict(named)
            after[dim] += way
            heapq.heappush(heap, (when, count, at, (after["x"], after["y"], after["z"]), dim, "link"))
            count += 1
            sends.append((dim, way))
        when = queue(("c", 1), now, size)
        heapq.heappush(heap, (when, count, at, rel, None, "core"))
        count += 1
        events.append((now, at, rel, kind, tuple(sends)))
    return pieces, events


def gather_kernel(nz, nx, ny, b_ref, e_ref, col_ref, row_ref, out_ref, blocks, energies,
                  send_sem, recv_sem, esend_sem, erecv_sem, own_sem):
    rows, width = b_ref.shape
    occ, aux = lax.axis_index("occ"), lax.axis_index("aux")
    z, x = occ // nx, occ % nx
    y, core = aux // CORES, aux % CORES
    sizes = {"x": nx, "y": ny, "z": nz}
    turn = 1 - 2 * core
    pieces, events = plan(rows, width, sizes)
    nocc = nz * nx

    def device(dx, dy, dz, dc):
        return (
            ((z + turn * dz + nz) % nz) * nx + (x + dx + nx) % nx,
            ((y + dy + ny) % ny) * CORES + (core + dc) % CORES,
        )

    barrier = pltpu.get_barrier_semaphore()
    for step in range(1, nocc):
        pl.semaphore_signal(barrier, inc=1, device_id=((occ + step) % nocc, aux), device_id_type=MESH)
    near = [(occ, (aux // CORES) * CORES + (core + 1) % CORES)]
    for way in (1, -1):
        if reach(ny)[way] >= 1:
            near.append(device(0, way, 0, 0))
    for target in near:
        pl.semaphore_signal(barrier, inc=1, device_id=target, device_id_type=MESH)
    pl.semaphore_wait(barrier, nocc - 1 + len(near))

    def columns(shard_aux):
        return pl.ds(pl.multiple_of(shard_aux * width, width), width)

    def place(at, shard):
        low, number, _ = pieces[at]
        return blocks.at[shard[0], pl.ds(low, number), columns(shard[1])]

    def source(at, shard, own):
        low, number, _ = pieces[at]
        return b_ref.at[pl.ds(low, number)] if own else place(at, shard)

    own_copy = pltpu.make_async_copy(b_ref, blocks.at[occ, :, columns(aux)], own_sem)
    own_copy.start()
    sent = []

    def send(at, shard, own, target):
        copy = pltpu.make_async_remote_copy(
            src_ref=source(at, shard, own), dst_ref=place(at, shard),
            send_sem=send_sem.at[len(sent)], recv_sem=recv_sem.at[at, shard[0], shard[1]],
            device_id=target, device_id_type=MESH,
        )
        copy.start()
        sent.append(copy)

    def arrive(at, shard):
        spot = place(at, shard)
        pltpu.make_async_remote_copy(
            src_ref=spot, dst_ref=spot, send_sem=own_sem, recv_sem=recv_sem.at[at, shard[0], shard[1]],
            device_id=(occ, aux), device_id_type=MESH,
        ).wait_recv()

    left = {}
    ready = []
    for _, at, rel, kind, _ in events:
        key = (rel[0] % nx, rel[2] % nz)
        left[key] = left.get(key, 0) + 1
    waiting = {"energies": True}
    small = []
    done = [False]

    def compute(key):
        block = device(-key[0], 0, -key[1], 0)[0]
        mine, other = blocks.at[occ], blocks.at[block]
        value = lax.dot_general(mine[...], other[...], (((1,), (1,)), ((), ())), preferred_element_type=jnp.float32)
        numer = 2.0 * value - value.T
        denom = col_ref[...] + row_ref[...] - e_ref[0:1, 0:1] - energies[block, 0:1, 0:1]
        amps = (numer / denom).astype(jnp.bfloat16)
        term = jnp.dot(amps, blocks[block, :, columns(aux)], preferred_element_type=jnp.float32)
        out_ref[...] = out_ref[...] + term if done[0] else term
        done[0] = True

    started = False
    for _, at, rel, kind, sends in events:
        dx, dy, dz = -rel[0], -rel[1], -rel[2]
        key = (rel[0] % nx, rel[2] % nz)
        if kind == "core":
            arrive(at, partner_shard(device, nz, nx, z, x, y, core, turn, dx, dy, dz, ny))
            rel_key = (rel[0] % nx, (-rel[2]) % nz)
            key = rel_key
        else:
            shard = device(dx, dy, dz, 0)
            if kind == "link":
                arrive(at, shard)
            for dim, way in sends:
                step = {"x": 0, "y": 0, "z": 0}
                step[dim] = way
                send(at, shard, kind == "own", device(step["x"], step["y"], step["z"], 0))
            send(at, shard, kind == "own", device(0, 0, 0, 1))
        left[key] -= 1
        if kind == "own" and not started and at == len(pieces) - 1:
            started = True
            keep = pltpu.make_async_copy(e_ref, energies.at[occ], esend_sem.at[0])
            keep.start()
            for step in range(1, nocc):
                copy = pltpu.make_async_remote_copy(
                    src_ref=e_ref, dst_ref=energies.at[occ], send_sem=esend_sem.at[step],
                    recv_sem=erecv_sem.at[occ], device_id=((occ + step) % nocc, aux), device_id_type=MESH,
                )
                copy.start()
                small.append(copy)
            keep.wait()
            own_copy.wait()
        if left[key] == 0:
            left[key] = -1
            ready.append(key)
            if (0, 0) in ready or done[0]:
                for one in ready:
                    if one != (0, 0) and waiting["energies"]:
                        waiting["energies"] = False
                        for step in range(1, nocc):
                            who = (occ + step) % nocc
                            pltpu.make_async_remote_copy(
                                src_ref=e_ref, dst_ref=energies.at[who], send_sem=own_sem,
                                recv_sem=erecv_sem.at[who], device_id=(occ, aux), device_id_type=MESH,
                            ).wait_recv()
                    compute(one)
                ready.clear()
    for copy in sent + small:
        copy.wait_send()


def partner_shard(device, nz, nx, z, x, y, core, turn, dx, dy, dz, ny):
    return (
        ((z - turn * dz + nz) % nz) * nx + (x + dx + nx) % nx,
        ((y + dy + ny) % ny) * CORES + (core + 1) % CORES,
    )


def gathered(three_index, occ_energy, vir_energy, nz, nx, ny):
    _, rows, width = three_index.shape
    nocc, naux = nz * nx, ny * CORES
    pieces, events = plan(rows, width, {"x": nx, "y": ny, "z": nz})
    copies = sum(len(e[4]) + 1 for e in events if e[3] != "core")
    energy = jnp.broadcast_to(occ_energy.reshape(1, 1), (8, 128))
    vmem = pl.BlockSpec(memory_space=pltpu.VMEM)
    out = pl.pallas_call(
        functools.partial(gather_kernel, nz, nx, ny),
        out_shape=jax.ShapeDtypeStruct((rows, width), jnp.float32),
        in_specs=[vmem] * 4,
        out_specs=vmem,
        scratch_shapes=[
            pltpu.VMEM((nocc, rows, naux * width), three_index.dtype),
            pltpu.VMEM((nocc, 8, 128), jnp.float32),
            pltpu.SemaphoreType.DMA((copies,)),
            pltpu.SemaphoreType.DMA((len(pieces), nocc, naux)),
            pltpu.SemaphoreType.DMA((nocc,)),
            pltpu.SemaphoreType.DMA((nocc,)),
            pltpu.SemaphoreType.DMA,
        ],
        compiler_params=pltpu.CompilerParams(
            collective_id=0, has_side_effects=True, vmem_limit_bytes=48 * 1024 * 1024
        ),
    )(three_index[0], energy, vir_energy[:, None], vir_energy[None, :])
    return out[None]


def pair_amps(rows_i, eps_i, rows_j, eps_j, vir_energy):
    partial_value = lax.dot_general(
        rows_i, rows_j, (((1,), (1,)), ((), ())), preferred_element_type=jnp.float32
    )
    occ_count = eps_i.shape[0]
    vir_count = vir_energy.shape[0]
    width = occ_count * vir_count
    four = partial_value.reshape(occ_count, vir_count, occ_count, vir_count)
    numer = (2.0 * four - jnp.transpose(four, (0, 3, 2, 1))).reshape(width, width)
    denom = (
        vir_energy[None, :, None, None]
        + vir_energy[None, None, None, :]
        - eps_i[:, None, None, None]
        - eps_j[None, None, :, None]
    ).reshape(width, width)
    share = width // lax.axis_size("aux")
    mine = lax.psum_scatter(numer, "aux", scatter_dimension=0, tiled=True)
    lower = lax.axis_index("aux") * share
    denom_rows = lax.dynamic_slice_in_dim(denom, lower, share, 0)
    amps_rows = (mine / denom_rows).astype(jnp.bfloat16)
    amps = lax.all_gather(amps_rows, "aux", axis=0, tiled=True)
    return amps


def apply_other(amps, rows_i):
    return lax.dot_general(
        amps, rows_i, (((0,), (0,)), ((), ())), preferred_element_type=jnp.float32
    )


def local(three_index, occ_energy, vir_energy):
    occ_count, vir_count, aux_count = three_index.shape
    cycle_size = lax.axis_size("occ")
    my_index = lax.axis_index("occ")
    all_energy = lax.all_gather(occ_energy, "occ", axis=0, tiled=True)
    own_rows = three_index.reshape(occ_count * vir_count, aux_count)

    def energy_of(step):
        block = (my_index - step + cycle_size) % cycle_size
        return lax.dynamic_slice_in_dim(all_energy, block * occ_count, occ_count)

    amps = pair_amps(own_rows, occ_energy, own_rows, occ_energy, vir_energy)
    gamma = jnp.dot(amps, own_rows, preferred_element_type=jnp.float32)
    half = cycle_size // 2
    carried = jnp.zeros_like(gamma)

    def cycle_step(step, state):
        rows_j, carried, gamma = state
        rows_j = from_behind(rows_j, "occ", 1)
        carried = from_behind(carried, "occ", 1)
        amps = pair_amps(own_rows, occ_energy, rows_j, energy_of(step), vir_energy)
        gamma = gamma + jnp.dot(amps, rows_j, preferred_element_type=jnp.float32)
        carried = carried + apply_other(amps, own_rows)
        return (rows_j, carried, gamma)

    rows_j, carried, gamma = lax.fori_loop(1, half, cycle_step, (own_rows, carried, gamma))
    rows_j = from_behind(rows_j, "occ", 1)
    amps = pair_amps(own_rows, occ_energy, rows_j, energy_of(half), vir_energy)
    gamma = gamma + jnp.dot(amps, rows_j, preferred_element_type=jnp.float32)
    returned = from_behind(carried, "occ", 1 - half)
    gamma = gamma + returned
    return gamma.reshape(occ_count, vir_count, aux_count)


def solution(mesh):
    nocc, naux = mesh.shape["occ"], mesh.shape["aux"]

    def either(three_index, occ_energy, vir_energy):
        _, rows, width = three_index.shape
        whole = nocc * naux * three_index.size * three_index.dtype.itemsize
        fits = whole <= GATHER_LIMIT and three_index.shape[0] == 1
        if fits and naux % CORES == 0 and nocc % 2 == 0:
            return gathered(three_index, occ_energy, vir_energy, nocc // 2, 2, naux // CORES)
        return local(three_index, occ_energy, vir_energy)

    return jax.shard_map(
        either,
        mesh=mesh,
        in_specs=(P("occ", None, "aux"), P("occ"), P()),
        out_specs=P("occ", None, "aux"),
        check_vma=False,
    )
```
